32 devices in a mesh: sample: 4 (over x, core), ctx: 8 (over z, y).
Axes of the slice: x: 2, y: 2, z: 4, core: 2. Of those that a mesh axis runs over, the one named last changes fastest.
Arguments:
- queries: bfloat16 [4096, 2048], P(('sample', 'ctx')), may hold values from -4 to 4
- experts: int32 [4096, 16], P(('sample', 'ctx')), may hold values from 0 to 63, all different within a row; in each aligned block of 128 rows (0 to 127, 128 to 255, ...) at most 64 rows name the same one
- gate: float32 [4096, 16], P(('sample', 'ctx')), may hold values from 0.05 to 1
- prefix_keys: bfloat16 [128, 1024], P('ctx'), may hold values from -8 to 8
- prefix_values: bfloat16 [128, 1024], P('ctx'), may hold values from -6 to 6
- d_out: bfloat16 [4096, 2048], P(('sample', 'ctx')), may hold values from -6 to 6
- lengths: int32 [4], replicated, may hold values from 128 to 1024
Outputs:
- attended: bfloat16 [4096, 2048], P(('sample', 'ctx'))
- query_grad: bfloat16 [4096, 2048], P(('sample', 'ctx'))
- gate_grad: float32 [4096, 16], P(('sample', 'ctx'))
- key_grad: float32 [128, 1024], P('ctx')
- value_grad: float32 [128, 1024], P('ctx')
The draws below stay inside these ranges and needn't reach their ends.
Inputs may be any that keep to these rules, and one draw needn't show every extreme that they name: `experts`: among the tokens of one device (aligned blocks of 128 tokens) no expert is picked more than 64 times, and some expert is picked exactly 64 times; a token's picks are distinct. Completion c holds tokens c * 1024 to (c + 1) * 1024 - 1; its first lengths[c] tokens are live.
All inputs are finite; a program needn't handle non-finite values.
Results may differ from the reference program's by a relative error of at most 0.012.
Values may be sent and summed in bfloat16 or wider, within the bound.
No kernel may reach another device: no remote copies, remote signals or barrier semaphores. Data moves between devices by JAX's collectives and lax.ppermute only.
A program may use at most 64 MiB of HBM per device.

```python
import math
import jax
import jax.numpy as jnp
import numpy as np
from jax import lax

HEAD = 128
KV_HEADS = 8
EXPERTS = 64
TOPK = 16
CLEN = 1024
CTOK = 128
CAP = 64
TOKENS = 4096
COMPLETIONS = 4
PREFIX = 128


def draw_prefix_keys(key, part):
    base = jax.random.normal(jax.random.fold_in(key, 7), (PREFIX, KV_HEADS * HEAD), jnp.float32)
    base = jnp.clip(base, -8.0, 8.0)
    return base.astype(jnp.bfloat16)


def draw_queries(key, part):
    inner = jax.random.fold_in(key, 3)
    base = jnp.clip(jax.random.normal(inner, (TOKENS, TOPK * HEAD), jnp.float32), -4.0, 4.0)
    return base.astype(jnp.bfloat16)


def touch_ends(values, stream_key, smallest, largest):
    spot = [jax.random.randint(jax.random.fold_in(stream_key, axis), (), 0, length) for axis, length in enumerate(values.shape)]
    longest = values.shape.index(max(values.shape))
    next_to = spot[:longest] + [(spot[longest] + 1) % values.shape[longest]] + spot[longest + 1:]
    return values.at[tuple(spot)].set(smallest).at[tuple(next_to)].set(largest)


def shard_levels(key, dims, split, smallest, top_value):
    loudness, own = 1.0, jax.random.fold_in(key, 6)
    for dim, parts in split:
        steps = jnp.exp(jax.random.uniform(jax.random.fold_in(own, dim), (parts,), jnp.float32, smallest / len(split), top_value / len(split)))
        loudness = loudness * jnp.repeat(steps, dims[dim] // parts).reshape([-1 if axis == dim else 1 for axis in range(len(dims))])
    return loudness


def deal_out(own_key, own, number, rows, count, top, reach, slope):
    order = jax.random.permutation(own_key, count)
    packed, common = shares(count, rows * top, reach, slope, True), shares(count, rows * top, reach, slope, False)
    places = jnp.arange(count)

    def named(tallies, offset_by):
        used = int((tallies > 0).sum())
        fixed = max(1, used // 4)
        passed = fixed + (places - fixed + offset_by * (used - fixed)) % max(1, count - fixed)
        return jnp.zeros((count,), jnp.int32).at[order[jnp.where(places < fixed, places, passed)]].set(jnp.asarray(tallies, jnp.int32))

    tallies = jnp.where(number % 4 == 0, named(packed, number // 4), named(common, number - number // 4 - 1))
    mixed = jax.random.permutation(jax.random.fold_in(own, 3), count)
    giver, taker = mixed[0:count // 2 * 2:2], mixed[1:count // 2 * 2:2]
    slack = jnp.minimum(tallies[giver] - 1, reach - tallies[taker]) // 2
    slack = jnp.where((giver == order[0]) | (taker == order[0]) | (tallies[taker] == 0), 0, jnp.maximum(slack, 0))
    passed = jax.random.randint(jax.random.fold_in(own, 4), (count // 2,), 0, 1 << 20) % (slack + 1)
    tallies = tallies.at[giver].add(-passed).at[taker].add(passed)
    members = jnp.searchsorted(jnp.cumsum(tallies), jnp.arange(rows * top), side="right").astype(jnp.int32)
    listing = members.reshape(top, rows).T
    listing = listing[jax.random.permutation(jax.random.fold_in(own, 1), rows)]
    offset_by = jax.random.randint(jax.random.fold_in(own, 2), (rows, 1), 0, top)
    return jnp.take_along_axis(listing, (jnp.arange(top)[None, :] + offset_by) % top, axis=1)


def shares(number_of, total, most, skew, full):
    portions = [(1 << 20) // math.isqrt(grade ** skew) + 1 for grade in range(1, number_of + 1)]
    largest = most if full else min(most, max(-(-total // number_of), total * portions[0] // sum(portions)))
    least = 1 if total - largest >= number_of - 1 else 0
    given, surplus = [largest] + [least] * (number_of - 1), total - largest - least * (number_of - 1)
    while surplus > 0:
        movable = [i for i in range(1, number_of) if given[i] < largest] or [i for i in range(1, number_of) if given[i] < most]
        pool, remaining = sum([portions[i] for i in movable]), surplus
        for i in movable:
            extra = min(most - given[i], max(1, remaining * portions[i] // pool), surplus)
            given[i] = given[i] + extra
            surplus = surplus - extra
    return np.array(given)


def noise(key, shape, deviation, most, pieces=(), held_as=jnp.bfloat16):
    values = jax.random.normal(key, shape, jnp.float32) * deviation
    if len(pieces) > 0:
        values = shard_levels(key, shape, pieces, -0.22, 0.18) * values
    return jnp.clip(values, min=-most, max=most).astype(held_as)


def setup_inputs(seed: int = 0) -> dict:
    key_list = jax.random.split(jax.random.key(seed), 8)
    queries = draw_queries(jax.random.fold_in(key_list[7], 71), 0)
    experts_keys = jax.random.split(jax.random.fold_in(key_list[1], 1), TOKENS // CTOK)
    experts_turns = jax.random.permutation(jax.random.fold_in(key_list[1], 3), TOKENS // CTOK)
    experts = jax.vmap(lambda own, number: deal_out(jax.random.fold_in(key_list[1], 2), own, number, CTOK, EXPERTS, TOPK, CAP, 2))(experts_keys, experts_turns).reshape((TOKENS, TOPK))
    gate = jnp.clip(jnp.exp(math.log(1.0) - 2.9957323 * jax.random.uniform(key_list[2], (TOKENS, TOPK), jnp.float32) ** shard_levels(key_list[2], (TOKENS, TOPK), ((0, 32),), -0.2, 0.2)), 0.05, 1.0)
    prefix_keys = draw_prefix_keys(jax.random.fold_in(key_list[7], 71), 0)
    prefix_values = noise(key_list[4], (PREFIX, KV_HEADS * HEAD), 1.0, 6.0, ((0, 8),))
    d_out = noise(key_list[5], (TOKENS, TOPK * HEAD), 1.0, 6.0, ((0, 32),))
    lengths = touch_ends(jax.random.randint(key_list[6], (COMPLETIONS,), CLEN // 8, CLEN + 1), jax.random.fold_in(key_list[6], 1), CLEN // 8, CLEN).astype(jnp.int32)
    return {"queries": queries, "experts": experts, "gate": gate, "prefix_keys": prefix_keys, "prefix_values": prefix_values, "d_out": d_out, "lengths": lengths}


def slot_index(experts):
    flat = experts.reshape(-1)
    picked = (flat[:, None] == jnp.arange(EXPERTS, dtype=jnp.int32)[None, :]).astype(jnp.int32)
    before = jnp.cumsum(picked, axis=0) - picked
    return (flat * CAP + jnp.sum(before * picked, axis=1)).astype(jnp.int32)


def to_low(value):
    return lax.optimization_barrier(value.astype(jnp.bfloat16)).astype(jnp.float32)


def reference(queries, experts, gate, prefix_keys, prefix_values, d_out, lengths):
    scale = HEAD ** -0.5
    width = KV_HEADS * HEAD
    group = EXPERTS * CAP // KV_HEADS
    keys = prefix_keys.astype(jnp.float32).reshape(PREFIX, KV_HEADS, HEAD)
    values = prefix_values.astype(jnp.float32).reshape(PREFIX, KV_HEADS, HEAD)
    token_ids = jnp.arange(TOKENS, dtype=jnp.int32)
    live = (token_ids % CLEN < lengths[token_ids // CLEN]).astype(jnp.float32)
    blocks = TOKENS // CTOK

    def step(carry, item):
        q_rows, expert_rows, gate_rows, cot_rows, live_rows = item
        slots = slot_index(expert_rows)
        q_buf = jnp.zeros((EXPERTS * CAP, HEAD), jnp.bfloat16).at[slots].set(q_rows.reshape(-1, HEAD))
        q_buf = q_buf.reshape(KV_HEADS, group, HEAD).astype(jnp.float32)
        score = jnp.einsum("hgd,phd->hgp", q_buf, keys) * scale
        high = jnp.max(score, axis=2)
        weight = jnp.exp(score - high[..., None])
        total = jnp.sum(weight, axis=2)
        output = jnp.einsum("hgp,phd->hgd", to_low(weight), values) / total[..., None]
        lse = high + jnp.log(total)
        o_rows = output.reshape(EXPERTS * CAP, HEAD)[slots].reshape(CTOK, TOPK, HEAD)
        cot = cot_rows.astype(jnp.float32).reshape(CTOK, TOPK, HEAD)
        factor = gate_rows * live_rows[:, None]
        result = (factor[..., None] * o_rows).reshape(CTOK, TOPK * HEAD).astype(jnp.bfloat16)
        gate_part = live_rows[:, None] * jnp.sum(o_rows * cot, axis=2)
        dout_rows = (factor[..., None] * cot).astype(jnp.bfloat16)
        dout_buf = jnp.zeros((EXPERTS * CAP, HEAD), jnp.bfloat16).at[slots].set(dout_rows.reshape(-1, HEAD))
        dout_buf = dout_buf.reshape(KV_HEADS, group, HEAD).astype(jnp.float32)
        delta = jnp.sum(dout_buf * output, axis=2)
        prob = jnp.exp(score - lse[..., None])
        dprob = jnp.einsum("hgd,phd->hgp", dout_buf, values)
        dscore = to_low(prob * (dprob - delta[..., None]))
        dq_buf = jnp.einsum("hgp,phd->hgd", dscore, keys) * scale
        key_part = jnp.einsum("hgp,hgd->phd", dscore, q_buf) * scale
        value_part = jnp.einsum("hgp,hgd->phd", to_low(prob), dout_buf)
        dq_rows = dq_buf.reshape(EXPERTS * CAP, HEAD)[slots].reshape(CTOK, TOPK * HEAD).astype(jnp.bfloat16)
        return (carry[0] + key_part, carry[1] + value_part), (result, dq_rows, gate_part)

    items = (queries.reshape(blocks, CTOK, TOPK * HEAD), experts.reshape(blocks, CTOK, TOPK),
             gate.reshape(blocks, CTOK, TOPK), d_out.reshape(blocks, CTOK, TOPK * HEAD),
             live.reshape(blocks, CTOK))
    start = (jnp.zeros((PREFIX, KV_HEADS, HEAD), jnp.float32), jnp.zeros((PREFIX, KV_HEADS, HEAD), jnp.float32))
    sums, stacked = lax.scan(step, start, items)
    attended = stacked[0].reshape(TOKENS, TOPK * HEAD)
    query_grad = stacked[1].reshape(TOKENS, TOPK * HEAD)
    gate_grad = stacked[2].reshape(TOKENS, TOPK)
    return attended, query_grad, gate_grad, sums[0].reshape(PREFIX, width), sums[1].reshape(PREFIX, width)
```

```python
import functools
import jax
import jax.numpy as jnp
from jax import lax
from jax.experimental import pallas as pl
from jax.experimental.pallas import tpu as pltpu
from jax.sharding import PartitionSpec as P

HEAD = 128
EXPERTS = 64
CLEN = 1024
SCALE = HEAD ** (-0.5)
LOG2E = 1.4426950408889634
F32 = jnp.float32
BF16 = jnp.bfloat16
AXES = ("sample", "ctx")
PICKS = 2


def grads_kernel(per_head, halves, info, q_ref, do_ref, ex_ref, gate_ref, *refs):
    blocks, (mine_ref, theirs_ref, prob_ref, ds_ref, gg_ref), scratch = refs[: 2 * halves], refs[2 * halves : 2 * halves + 5], refs[2 * halves + 5 :]
    kp, vp, q4, do4, p2, ds2 = scratch
    tokens, topk = ex_ref.shape
    own = blocks[0].shape[0] // 2
    total = 2 * halves * own
    pairs = kp.shape[1] // HEAD
    for b, ref in enumerate(blocks):
        for h in range(2 * pairs):
            rows = pl.ds((h % 2) * total + b * own, own)
            cols = pl.ds((h // 2) * HEAD, HEAD)
            kp[rows, cols] = ref[:own, h * HEAD : (h + 1) * HEAD]
            vp[rows, cols] = ref[own:, h * HEAD : (h + 1) * HEAD]
    head = ex_ref[...] // per_head
    pair = head // 2
    head_t = jnp.transpose(head.astype(F32))
    odd_t = head_t - 2.0 * jnp.floor(head_t * 0.5)
    live = (lax.broadcasted_iota(jnp.int32, (topk, tokens), 1) < info[0]).astype(F32)
    factor = jnp.transpose(gate_ref[...]) * live
    gates = []
    for c in range(topk // PICKS):
        lo, hi = c * PICKS * tokens, (c + 1) * PICKS * tokens
        odd, fac = [], []
        for k in range(c * PICKS, (c + 1) * PICKS):
            rows = pl.ds(k * tokens, tokens)
            q = q_ref[:, k * HEAD : (k + 1) * HEAD]
            do = do_ref[:, k * HEAD : (k + 1) * HEAD]
            spread = jnp.broadcast_to(pair[:, k : k + 1], (tokens, HEAD))
            for j in range(pairs):
                hot = jnp.where(spread == j, 1.0, 0.0).astype(BF16)
                q4[rows, j * HEAD : (j + 1) * HEAD] = q * hot
                do4[rows, j * HEAD : (j + 1) * HEAD] = do * hot
            odd.append(odd_t[k : k + 1, :])
            fac.append(factor[k : k + 1, :])
        odd = jnp.concatenate(odd, axis=1)
        fac = jnp.concatenate(fac, axis=1)
        is_odd = odd > 0.5
        nt = (((1,), (1,)), ((), ()))
        s2 = lax.dot_general(kp[...], q4[lo:hi, :], nt, preferred_element_type=F32)
        s = jnp.where(is_odd, s2[total:], s2[:total])
        d2 = lax.dot_general(vp[...], do4[lo:hi, :], nt, preferred_element_type=F32)
        dp = jnp.where(is_odd, d2[total:], d2[:total])
        high = jnp.max(s, axis=0, keepdims=True)
        e = jnp.exp2((s - high) * (SCALE * LOG2E))
        prob = e * (1.0 / jnp.sum(e, axis=0, keepdims=True))
        delta = jnp.sum(prob * dp, axis=0, keepdims=True)
        gates.append(delta)
        pf = prob * fac
        ds = pf * (dp - delta)
        prob_ref[:, lo:hi] = pf.astype(BF16)
        ds_ref[:, lo:hi] = ds.astype(BF16)
        p2[:total, lo:hi] = jnp.where(is_odd, 0.0, pf).astype(BF16)
        p2[total:, lo:hi] = jnp.where(is_odd, pf, 0.0).astype(BF16)
        ds2[:total, lo:hi] = jnp.where(is_odd, 0.0, ds).astype(BF16)
        ds2[total:, lo:hi] = jnp.where(is_odd, ds, 0.0).astype(BF16)
    gg = jnp.concatenate([g[:, i * tokens : (i + 1) * tokens] for g in gates for i in range(PICKS)], axis=0)
    gg_ref[...] = jnp.transpose(gg * live)
    for offset, (left, right, times) in enumerate(((ds2, q4, SCALE), (p2, do4, 1.0))):
        out = jnp.dot(left[...], right[...], preferred_element_type=F32) * times
        for b in range(2 * halves):
            ref = mine_ref if b < halves else theirs_ref
            rows = pl.ds((b % halves) * 2 * own + offset * own, own)
            for h in range(2 * pairs):
                piece = out[(h % 2) * total + b * own : (h % 2) * total + (b + 1) * own, (h // 2) * HEAD : (h // 2 + 1) * HEAD]
                ref[rows, h * HEAD : (h + 1) * HEAD] = piece.astype(ref.dtype)


def rows_kernel(per_head, halves, ex_ref, prob_ref, ds_ref, *refs):
    blocks, (att_ref, dq_ref), (kt, vt) = refs[: 2 * halves], refs[2 * halves : 2 * halves + 2], refs[2 * halves + 2 :]
    tokens, topk = ex_ref.shape
    own = blocks[0].shape[0] // 2
    total = 2 * halves * own
    pairs = kt.shape[1] // total
    for h in range(2 * pairs):
        cols = slice(h * HEAD, (h + 1) * HEAD)
        for dst, part in ((kt, slice(0, own)), (vt, slice(own, 2 * own))):
            whole = jnp.concatenate([ref[part, cols] for ref in blocks], axis=0)
            dst[(h % 2) * HEAD : (h % 2 + 1) * HEAD, (h // 2) * total : (h // 2 + 1) * total] = jnp.transpose(whole)
    head_t = jnp.transpose((ex_ref[...] // per_head).astype(F32))
    pair_t = jnp.floor(head_t * 0.5)
    odd_t = head_t - 2.0 * pair_t
    for c in range(topk // PICKS):
        lo, hi = c * PICKS * tokens, (c + 1) * PICKS * tokens
        ks = range(c * PICKS, (c + 1) * PICKS)
        pair = jnp.concatenate([pair_t[k : k + 1, :] for k in ks], axis=1)
        is_odd = jnp.concatenate([odd_t[k : k + 1, :] for k in ks], axis=1) > 0.5
        hots = [jnp.broadcast_to(jnp.where(pair == j, 1.0, 0.0), (16, hi - lo)).astype(BF16) for j in range(pairs)]
        for src, left, out_ref, times in ((prob_ref, vt, att_ref, None), (ds_ref, kt, dq_ref, SCALE)):
            val = src[:, lo:hi].reshape(total // 16, 16, hi - lo)
            wide = jnp.concatenate([(val * hot[None]).reshape(total, hi - lo) for hot in hots], axis=0)
            out2 = jnp.dot(left[...], wide, preferred_element_type=F32)
            out = jnp.where(is_odd, out2[HEAD:], out2[:HEAD])
            if times is not None:
                out = out * times
            out = out.astype(BF16)
            for i, k in enumerate(ks):
                out_ref[:, k * HEAD : (k + 1) * HEAD] = jnp.transpose(out[:, i * tokens : (i + 1) * tokens])


def gather_pairs(n_sample, n_ctx, first, second):
    out = []
    for s in range(n_sample):
        for j in range(n_ctx):
            o = second if s % 2 else first
            src = j ^ o if n_ctx & (n_ctx - 1) == 0 else (j + o) % n_ctx
            out.append((s * n_ctx + src, s * n_ctx + j))
    return out


def swap_pairs(n_sample, n_ctx, bit):
    return [(s * n_ctx + j, (s ^ bit) * n_ctx + j) for s in range(n_sample) for j in range(n_ctx)]


def local(queries, experts, gate, prefix_keys, prefix_values, d_out, lengths):
    n_sample, n_ctx = lax.axis_size("sample"), lax.axis_size("ctx")
    tokens, topk = experts.shape
    own, width = prefix_keys.shape
    heads = width // HEAD
    per_head = EXPERTS // heads
    total = own * n_ctx
    halves = n_ctx // 2
    picked = tokens * topk
    pairs = heads // 2
    assert n_ctx % 2 == 0 and n_sample & (n_sample - 1) == 0 and n_sample > 1 and CLEN % tokens == 0

    begin = (lax.axis_index("sample") * n_ctx + lax.axis_index("ctx")) * tokens
    count = lax.dynamic_index_in_dim(lengths, begin // CLEN, 0, keepdims=True) - begin % CLEN

    offsets = list(range(1, n_ctx)) + [0]
    firsts, seconds = offsets[0::2], offsets[1::2]
    routes = [gather_pairs(n_sample, n_ctx, a, b) for a, b in zip(firsts, seconds, strict=True)]
    swap = swap_pairs(n_sample, n_ctx, 1)
    block = jnp.concatenate([prefix_keys, prefix_values], axis=0)
    got = [lax.ppermute(block, AXES, r) for r in routes]
    other = [lax.ppermute(g, AXES, swap) for g in got]
    blocks = got + other

    vmem = pl.BlockSpec(memory_space=pltpu.VMEM)
    smem = pl.BlockSpec(memory_space=pltpu.SMEM)
    flops = 2 * 4 * picked * total * width
    mine, theirs, prob, ds, gate_grad = pl.pallas_call(
        functools.partial(grads_kernel, per_head, halves),
        out_shape=(
            jax.ShapeDtypeStruct((halves * 2 * own, width), F32),
            jax.ShapeDtypeStruct((halves * 2 * own, width), BF16),
            jax.ShapeDtypeStruct((total, picked), BF16),
            jax.ShapeDtypeStruct((total, picked), BF16),
            jax.ShapeDtypeStruct((tokens, topk), F32),
        ),
        in_specs=[smem] + [vmem] * (4 + 2 * halves),
        out_specs=[vmem] * 5,
        scratch_shapes=[
            pltpu.VMEM((2 * total, pairs * HEAD), BF16),
            pltpu.VMEM((2 * total, pairs * HEAD), BF16),
            pltpu.VMEM((picked, pairs * HEAD), BF16),
            pltpu.VMEM((picked, pairs * HEAD), BF16),
            pltpu.VMEM((2 * total, picked), BF16),
            pltpu.VMEM((2 * total, picked), BF16),
        ],
        cost_estimate=pl.CostEstimate(flops=flops, bytes_accessed=4 << 20, transcendentals=picked * total),
        name="grads",
    )(count, queries, d_out, experts, gate, *blocks)

    attended, query_grad = pl.pallas_call(
        functools.partial(rows_kernel, per_head, halves),
        out_shape=(
            jax.ShapeDtypeStruct(queries.shape, BF16),
            jax.ShapeDtypeStruct(queries.shape, BF16),
        ),
        in_specs=[vmem] * (3 + 2 * halves),
        out_specs=[vmem] * 2,
        scratch_shapes=[
            pltpu.VMEM((2 * HEAD, pairs * total), BF16),
            pltpu.VMEM((2 * HEAD, pairs * total), BF16),
        ],
        cost_estimate=pl.CostEstimate(flops=flops // 2, bytes_accessed=2 << 20, transcendentals=0),
        name="rows",
    )(experts, prob, ds, *blocks)

    from_other = lax.ppermute(theirs, AXES, swap).astype(F32)
    parts = []
    for m, route in enumerate(routes):
        rows = slice(m * 2 * own, (m + 1) * 2 * own)
        back = [(dst, src) for src, dst in route]
        parts.append(lax.ppermute((mine[rows] + from_other[rows]).astype(BF16), AXES, back))
    share = sum(p.astype(F32) for p in parts)
    share = share + lax.ppermute(share, AXES, swap)
    bit = 2
    while bit < n_sample:
        share = share + lax.ppermute(share, AXES, swap_pairs(n_sample, n_ctx, bit))
        bit *= 2
    return (attended, query_grad, gate_grad, share[:own], share[own:])


def solution(mesh):
    row = P(("sample", "ctx"), None)
    return jax.shard_map(
        local,
        mesh=mesh,
        in_specs=(row, row, row, P("ctx", None), P("ctx", None), row, P()),
        out_specs=(row, row, row, P("ctx", None), P("ctx", None)),
        check_vma=False,
    )
```

```python
import functools
import jax
import jax.numpy as jnp
from jax import lax
from jax.experimental import pallas as pl
from jax.experimental.pallas import tpu as pltpu
from jax.sharding import PartitionSpec as P

HEAD = 128
EXPERTS = 64
CLEN = 1024
SCALE = HEAD ** (-0.5)
LOG2E = 1.4426950408889634
F32 = jnp.float32
BF16 = jnp.bfloat16
AXES = ("sample", "ctx")
PICKS = 2


def grads_kernel(per_head, halves, begin_ref, lengths_ref, q_ref, do_ref, ex_ref, gate_ref, *refs):
    blocks, (mine_ref, theirs_ref, prob_ref, ds_ref, gg_ref), scratch = refs[: 2 * halves], refs[2 * halves : 2 * halves + 5], refs[2 * halves + 5 :]
    kp, vp, q4, do4, p2, ds2 = scratch
    topk, tokens = ex_ref.shape
    own = blocks[0].shape[0] // 2
    total = 2 * halves * own
    pairs = kp.shape[1] // HEAD
    begin = begin_ref[0]
    count = lengths_ref[begin // CLEN] - begin % CLEN
    for b, ref in enumerate(blocks):
        for h in range(2 * pairs):
            rows = pl.ds((h % 2) * total + b * own, own)
            cols = pl.ds((h // 2) * HEAD, HEAD)
            kp[rows, cols] = ref[:own, h * HEAD : (h + 1) * HEAD]
            vp[rows, cols] = ref[own:, h * HEAD : (h + 1) * HEAD]
    head_t = jnp.floor(ex_ref[...].astype(F32) * (1.0 / per_head))
    pair_t = jnp.floor(head_t * 0.5)
    odd_t = head_t - 2.0 * pair_t
    pair = jnp.transpose(pair_t)
    live = (lax.broadcasted_iota(jnp.int32, (topk, tokens), 1) < count).astype(F32)
    factor = gate_ref[...] * live
    gates = []
    for c in range(topk // PICKS):
        lo, hi = c * PICKS * tokens, (c + 1) * PICKS * tokens
        odd, fac = [], []
        for k in range(c * PICKS, (c + 1) * PICKS):
            rows = pl.ds(k * tokens, tokens)
            q = q_ref[:, k * HEAD : (k + 1) * HEAD]
            do = do_ref[:, k * HEAD : (k + 1) * HEAD]
            spread = jnp.broadcast_to(pair[:, k : k + 1], (tokens, HEAD))
            for j in range(pairs):
                hot = jnp.where(spread == j, 1.0, 0.0).astype(BF16)
                q4[rows, j * HEAD : (j + 1) * HEAD] = q * hot
                do4[rows, j * HEAD : (j + 1) * HEAD] = do * hot
            odd.append(odd_t[k : k + 1, :])
            fac.append(factor[k : k + 1, :])
        odd = jnp.concatenate(odd, axis=1)
        fac = jnp.concatenate(fac, axis=1)
        is_odd = odd > 0.5
        nt = (((1,), (1,)), ((), ()))
        s2 = lax.dot_general(kp[...], q4[lo:hi, :], nt, preferred_element_type=F32)
        s = jnp.where(is_odd, s2[total:], s2[:total])
        d2 = lax.dot_general(vp[...], do4[lo:hi, :], nt, preferred_element_type=F32)
        dp = jnp.where(is_odd, d2[total:], d2[:total])
        high = jnp.max(s, axis=0, keepdims=True)
        e = jnp.exp2((s - high) * (SCALE * LOG2E))
        prob = e * (1.0 / jnp.sum(e, axis=0, keepdims=True))
        delta = jnp.sum(prob * dp, axis=0, keepdims=True)
        gates.append(delta)
        pf = prob * fac
        ds = pf * (dp - delta)
        prob_ref[:, lo:hi] = pf.astype(BF16)
        ds_ref[:, lo:hi] = ds.astype(BF16)
        p2[:total, lo:hi] = jnp.where(is_odd, 0.0, pf).astype(BF16)
        p2[total:, lo:hi] = jnp.where(is_odd, pf, 0.0).astype(BF16)
        ds2[:total, lo:hi] = jnp.where(is_odd, 0.0, ds).astype(BF16)
        ds2[total:, lo:hi] = jnp.where(is_odd, ds, 0.0).astype(BF16)
    gg = jnp.concatenate([g[:, i * tokens : (i + 1) * tokens] for g in gates for i in range(PICKS)], axis=0)
    gg_ref[...] = gg * live
    for offset, (left, right, times) in enumerate(((ds2, q4, SCALE), (p2, do4, 1.0))):
        out = jnp.dot(left[...], right[...], preferred_element_type=F32) * times
        for b in range(2 * halves):
            ref = mine_ref if b < halves else theirs_ref
            rows = pl.ds((b % halves) * 2 * own + offset * own, own)
            for h in range(2 * pairs):
                piece = out[(h % 2) * total + b * own : (h % 2) * total + (b + 1) * own, (h // 2) * HEAD : (h // 2 + 1) * HEAD]
                ref[rows, h * HEAD : (h + 1) * HEAD] = piece.astype(ref.dtype)


def rows_kernel(per_head, halves, part, times, ex_ref, src_ref, *refs):
    blocks, out_ref, left = refs[: 2 * halves], refs[2 * halves], refs[2 * halves + 1]
    topk, tokens = ex_ref.shape
    own = blocks[0].shape[0] // 2
    total = 2 * halves * own
    pairs = left.shape[1] // total
    for h in range(2 * pairs):
        whole = jnp.concatenate([ref[part * own : (part + 1) * own, h * HEAD : (h + 1) * HEAD] for ref in blocks], axis=0)
        left[(h % 2) * HEAD : (h % 2 + 1) * HEAD, (h // 2) * total : (h // 2 + 1) * total] = jnp.transpose(whole)
    head_t = jnp.floor(ex_ref[...].astype(F32) * (1.0 / per_head))
    pair_t = jnp.floor(head_t * 0.5)
    odd_t = head_t - 2.0 * pair_t
    for c in range(topk // PICKS):
        lo, hi = c * PICKS * tokens, (c + 1) * PICKS * tokens
        ks = range(c * PICKS, (c + 1) * PICKS)
        pair = jnp.concatenate([pair_t[k : k + 1, :] for k in ks], axis=1)
        is_odd = jnp.concatenate([odd_t[k : k + 1, :] for k in ks], axis=1) > 0.5
        hots = [jnp.broadcast_to(jnp.where(pair == j, 1.0, 0.0), (16, hi - lo)).astype(BF16) for j in range(pairs)]
        val = src_ref[:, lo:hi].reshape(total // 16, 16, hi - lo)
        wide = jnp.concatenate([(val * hot[None]).reshape(total, hi - lo) for hot in hots], axis=0)
        out2 = jnp.dot(left[...], wide, preferred_element_type=F32)
        out = jnp.where(is_odd, out2[HEAD:], out2[:HEAD])
        if times is not None:
            out = out * times
        out = out.astype(BF16)
        for i, k in enumerate(ks):
            out_ref[:, k * HEAD : (k + 1) * HEAD] = jnp.transpose(out[:, i * tokens : (i + 1) * tokens])


def gather_pairs(n_sample, n_ctx, first, second):
    walk = list(range(0, n_ctx, 2)) + list(range(n_ctx - 1, 0, -2))
    place = {j: i for i, j in enumerate(walk)}
    out = []
    for s in range(n_sample):
        for j in range(n_ctx):
            o = second if s % 2 else first
            out.append((s * n_ctx + walk[(place[j] + o) % n_ctx], s * n_ctx + j))
    return out


def swap_pairs(n_sample, n_ctx, bit):
    return [(s * n_ctx + j, (s ^ bit) * n_ctx + j) for s in range(n_sample) for j in range(n_ctx)]


def local(queries, experts, gate, prefix_keys, prefix_values, d_out, lengths):
    n_sample, n_ctx = lax.axis_size("sample"), lax.axis_size("ctx")
    tokens, topk = experts.shape
    own, width = prefix_keys.shape
    heads = width // HEAD
    per_head = EXPERTS // heads
    total = own * n_ctx
    halves = n_ctx // 2
    picked = tokens * topk
    pairs = heads // 2
    assert n_ctx % 2 == 0 and n_sample & (n_sample - 1) == 0 and n_sample > 1 and CLEN % tokens == 0

    begin = (lax.axis_index("sample") * n_ctx + lax.axis_index("ctx")) * tokens

    near_first = sorted(range(n_ctx), key=lambda o: (min(o, n_ctx - o), o))
    firsts = (near_first[: halves - 1] + near_first[-1:])[::-1]
    seconds = near_first[halves - 1 : -1][::-1]
    routes = [gather_pairs(n_sample, n_ctx, a, b) for a, b in zip(firsts, seconds, strict=True)]
    swap = swap_pairs(n_sample, n_ctx, 1)
    block = jnp.concatenate([prefix_keys, prefix_values], axis=0)
    got = [lax.ppermute(block, AXES, r) for r in routes]
    other = [lax.ppermute(g, AXES, swap) for g in got]
    blocks = got + other

    vmem = pl.BlockSpec(memory_space=pltpu.VMEM)
    smem = pl.BlockSpec(memory_space=pltpu.SMEM)
    flops = 2 * 4 * picked * total * width
    mine, theirs, prob, ds, gate_grad = pl.pallas_call(
        functools.partial(grads_kernel, per_head, halves),
        out_shape=(
            jax.ShapeDtypeStruct((halves * 2 * own, width), F32),
            jax.ShapeDtypeStruct((halves * 2 * own, width), BF16),
            jax.ShapeDtypeStruct((total, picked), BF16),
            jax.ShapeDtypeStruct((total, picked), BF16),
            jax.ShapeDtypeStruct((topk, tokens), F32),
        ),
        in_specs=[smem] * 2 + [vmem] * (4 + 2 * halves),
        out_specs=[vmem] * 5,
        scratch_shapes=[
            pltpu.VMEM((2 * total, pairs * HEAD), BF16),
            pltpu.VMEM((2 * total, pairs * HEAD), BF16),
            pltpu.VMEM((picked, pairs * HEAD), BF16),
            pltpu.VMEM((picked, pairs * HEAD), BF16),
            pltpu.VMEM((2 * total, picked), BF16),
            pltpu.VMEM((2 * total, picked), BF16),
        ],
        cost_estimate=pl.CostEstimate(flops=flops, bytes_accessed=4 << 20, transcendentals=picked * total),
        name="grads",
    )(begin.reshape(1), lengths, queries, d_out, experts.T, gate.T, *blocks)

    def rows(part, times, src, name):
        return pl.pallas_call(
            functools.partial(rows_kernel, per_head, halves, part, times),
            out_shape=jax.ShapeDtypeStruct(queries.shape, BF16),
            in_specs=[vmem] * (2 + 2 * halves),
            out_specs=vmem,
            scratch_shapes=[pltpu.VMEM((2 * HEAD, pairs * total), BF16)],
            cost_estimate=pl.CostEstimate(flops=flops // 4, bytes_accessed=2 << 20, transcendentals=0),
            name=name,
        )(experts.T, src, *blocks)

    attended = rows(1, None, prob, "attended")
    query_grad = rows(0, SCALE, ds, "query_grad")

    from_other = lax.ppermute(theirs, AXES, swap).astype(F32)
    parts = []
    for m, route in enumerate(routes):
        rows = slice(m * 2 * own, (m + 1) * 2 * own)
        back = [(dst, src) for src, dst in route]
        parts.append(lax.ppermute((mine[rows] + from_other[rows]).astype(BF16), AXES, back))
    share = sum(p.astype(F32) for p in parts)
    share = share + lax.ppermute(share, AXES, swap)
    bit = 2
    while bit < n_sample:
        share = share + lax.ppermute(share, AXES, swap_pairs(n_sample, n_ctx, bit))
        bit *= 2
    return (attended, query_grad, gate_grad.T, share[:own], share[own:])


def solution(mesh):
    row = P(("sample", "ctx"), None)
    return jax.shard_map(
        local,
        mesh=mesh,
        in_specs=(row, row, row, P("ctx", None), P("ctx", None), row, P()),
        out_specs=(row, row, row, P("ctx", None), P("ctx", None)),
        check_vma=False,
    )
```
